32 devices in a mesh: grp: 2 (over core), ep: 16 (over z, y, x).
Axes of the slice: x: 2, y: 2, z: 4, core: 2. Of those that a mesh axis runs over, the one named last changes fastest.
Arguments:
- out_grad: bfloat16 [16384, 2048], P(('grp', 'ep')), may hold values from -0.5 to 0.5
- probs: float32 [16384, 8], P(('grp', 'ep')), may hold values from 0.02 to 0.5
- dest: int32 [16384, 8], P(('grp', 'ep')), may hold values from -1 to 49151, as said below
- replica_owner: int32 [2, 16], P('grp'), may hold values from 0 to 15, as said below
- gate_up: bfloat16 [98304, 1536], P(('grp', 'ep')), may hold values from -6 to 6
Outputs:
- d_down: float32 [16, 768, 2048], P('ep', None, 'grp')
The draws below stay inside these ranges and needn't reach their ends.
Inputs may be any that keep to these rules, and one draw needn't show every extreme that they name: `dest`: copies of one token name distinct rows; a device's copies to slot buffer (j, s) fill the rows of that buffer's block for the device, which is the device's ep index times 96 onward, from its start without gaps; in every draw some device fills its block of some buffer, all 96 rows, and copies beyond a block are dropped. `replica_owner`: each entry names an expert that has its primary slot on that ep index of the group.
All inputs are finite; a program needn't handle non-finite values.
Results may differ from the reference program's by a relative error of at most 0.005.
Values may be sent and summed in bfloat16 or wider, within the bound.
A program may use at most 128 MiB of HBM per device.

```python
import math
import jax
import jax.numpy as jnp
from jax import lax

D = 2048
H = 768
TOP = 8
TOK_DEV = 512
EXPERTS = 16
HOT = 4
CAP = 1536
C_SRC = 96
TOKEN_TOTAL = 16384
SLOT_ROWS = 98304
N_GRP = 2
N_EP = 16


def plan_group(group_key):
    first, second_replica, third = jax.random.split(group_key, 3)
    experts = jnp.arange(EXPERTS, dtype=jnp.int32)
    order = jax.random.permutation(first, EXPERTS).astype(jnp.int32)
    hotness = jnp.zeros((EXPERTS,), jnp.int32).at[order[:HOT]].set(1)
    owners = order[jax.random.randint(second_replica, (EXPERTS,), 0, HOT)]
    bits = jax.random.randint(third, (EXPERTS * TOK_DEV, EXPERTS), 0, 1 << 20)
    score = bits * (1 + 2 * hotness)[None, :] * 64 + experts[None, :]
    unused, chosen_experts = lax.top_k(score, TOP)
    chosen_experts = chosen_experts.astype(jnp.int32).reshape(EXPERTS, TOK_DEV * TOP)
    onehot = (chosen_experts[:, :, None] == experts[None, None, :]).astype(jnp.int32)
    before = jnp.cumsum(onehot, axis=1) - onehot
    count = jnp.sum(before * onehot, axis=2)
    match_flags = (owners[None, :] == experts[:, None]).astype(jnp.int32)
    slot_count = 1 + jnp.sum(match_flags, axis=1)
    ranks = jnp.cumsum(match_flags, axis=1) * match_flags
    token_share = slot_count[chosen_experts]
    turn = count % token_share
    place = count // token_share
    picked = jnp.sum(experts[None, None, :] * (ranks[chosen_experts] == turn[:, :, None]).astype(jnp.int32), axis=2)
    device = jnp.where(turn == 0, chosen_experts, picked)
    second_slot = jnp.where(turn == 0, 0, 1)
    source = experts[:, None]
    target = device * 2 * CAP + second_slot * CAP + source * C_SRC + place
    target = jnp.where(place < C_SRC, target, -1)
    return (owners, target.reshape(EXPERTS * TOK_DEV, TOP))


def plan_all(key):
    base = jax.random.fold_in(key, 7)
    keys = jax.random.split(base, N_GRP)
    owners, targets = jax.vmap(plan_group)(keys)
    return (owners.astype(jnp.int32), targets.reshape(N_GRP * EXPERTS * TOK_DEV, TOP).astype(jnp.int32))


def draw_dest(key, part):
    owners, targets = plan_all(key)
    return targets


def draw_replica_owner(key, part):
    owners, targets = plan_all(key)
    return owners


def block_levels(stream_key, dims, pieces, low, top_value):
    def one(axis_at, shards_of):
        heights = jax.random.uniform(jax.random.fold_in(jax.random.fold_in(stream_key, 6), axis_at), (shards_of,), jnp.float32, low / len(pieces), top_value / len(pieces))
        return jnp.repeat(jnp.exp(heights), dims[axis_at] // shards_of).reshape((-1,) + (1,) * (len(dims) - axis_at - 1))

    level = one(*pieces[0])
    for cut in pieces[1:]:
        level = level * one(*cut)
    return level


def bell_draw(key, dims, spread, reach, cuts=(), kind=jnp.bfloat16):
    drawn = jax.random.normal(key, dims, jnp.float32) * spread
    if len(cuts) > 0:
        drawn = block_levels(key, dims, cuts, -0.22, 0.18) * drawn
    return jnp.clip(drawn, min=-reach, max=reach).astype(kind)


def setup_inputs(seed: int = 0) -> dict:
    arg_keys = jax.random.split(jax.random.key(seed), 6)
    out_grad = bell_draw(arg_keys[0], (TOKEN_TOTAL, D), 0.08, 0.5, ((0, 32),))
    probs = jnp.clip(jnp.exp(math.log(0.5) - 3.218876 * jax.random.uniform(arg_keys[1], (TOKEN_TOTAL, TOP), jnp.float32) ** block_levels(arg_keys[1], (TOKEN_TOTAL, TOP), ((0, 32),), -0.2, 0.2)), 0.02, 0.5)
    dest = draw_dest(jax.random.fold_in(arg_keys[5], 71), 0)
    replica_owner = draw_replica_owner(jax.random.fold_in(arg_keys[5], 71), 0)
    gate_up = bell_draw(arg_keys[4], (SLOT_ROWS, 2 * H), 1.0, 6.0, ((0, 32),))
    return {"out_grad": out_grad, "probs": probs, "dest": dest, "replica_owner": replica_owner, "gate_up": gate_up}


def reference(out_grad, probs, dest, replica_owner, gate_up):
    group_rows = 2 * N_EP * CAP
    group_tokens = N_EP * TOK_DEV
    total = jnp.zeros((N_EP, H, D), jnp.float32)
    for group in range(N_GRP):
        lower = group * group_tokens
        grad_rows = out_grad[lower:lower + group_tokens]
        flat_weights = probs[lower:lower + group_tokens].astype(jnp.float32).reshape(-1)
        targets = dest[lower:lower + group_tokens].astype(jnp.int32)
        index = jnp.where(targets >= 0, targets, group_rows).reshape(-1).astype(jnp.int32)
        copy_of = jnp.full((group_rows,), -1, jnp.int32).at[index].set(
            jnp.arange(group_tokens * TOP, dtype=jnp.int32), mode="drop")
        owners = replica_owner[group].astype(jnp.int32)
        row_start = group * group_rows

        def per_device(device, carry):
            device = jnp.asarray(device).astype(jnp.int32)
            base = (device * 2 * CAP).astype(jnp.int32)
            rows = lax.dynamic_slice_in_dim(copy_of, base, 2 * CAP, 0)
            safe = jnp.maximum(rows, 0).astype(jnp.int32)
            weight = jnp.where(rows >= 0, flat_weights[safe], jnp.zeros_like(flat_weights[safe]))
            picked = grad_rows[(safe // TOP).astype(jnp.int32)].astype(jnp.float32)
            grads = (weight[:, None] * picked).astype(jnp.bfloat16)
            saved = lax.dynamic_slice_in_dim(gate_up, (base + row_start).astype(jnp.int32), 2 * CAP, 0)
            act = (jax.nn.silu(saved[:, :H].astype(jnp.float32)) * saved[:, H:].astype(jnp.float32)).astype(jnp.bfloat16)
            tile_main = jnp.dot(act[:CAP].T, grads[:CAP], preferred_element_type=jnp.float32).astype(jnp.bfloat16)
            tile_copy = jnp.dot(act[CAP:].T, grads[CAP:], preferred_element_type=jnp.float32).astype(jnp.bfloat16)
            tile_main, tile_copy = lax.optimization_barrier((tile_main, tile_copy))
            carry = carry.at[device].add(tile_main.astype(jnp.float32))
            carry = carry.at[owners[device]].add(tile_copy.astype(jnp.float32))
            return carry

        total = lax.fori_loop(0, N_EP, per_device, total)
    return total
```

```python
import functools

import jax
import jax.numpy as jnp
from jax import lax
from jax.experimental import pallas as pl
from jax.experimental.pallas import tpu as pltpu
from jax.sharding import PartitionSpec as P

MESH = pl.DeviceIdType.MESH
LINE = 4
CHUNKS = 2
ACT_ROWS = 256


def dispatch_kernel(
    n_in, per_src, top,
    meta_hbm, og_hbm, gu_hbm, tiles_ref,
    tok, metas, sel, wgt, outb, inb, act_t, gubuf,
    ld_sem, gu_sem, zsend, zrecv, gsend, grecv, lsem,
):
    e = lax.axis_index("ep")
    z = e // n_in
    p = e % n_in
    cols = tok.shape[3]
    hidden = act_t.shape[1]
    cap = act_t.shape[2]
    block = 2 * per_src
    tokens = tok.shape[2]

    m = ((z + 1) // 2) % 2
    far, rev = (z + 2) % 4, 3 - z
    order = [z, z + 1 - 2 * (z % 2), (1 - m) * far + m * rev, (1 - m) * rev + m * far]

    def load(c):
        return pltpu.make_async_copy(
            og_hbm.at[:, pl.ds(c * cols, cols)], tok.at[c, z], ld_sem.at[c])

    def load_meta():
        return pltpu.make_async_copy(meta_hbm, metas.at[z], ld_sem.at[CHUNKS])

    def gu_load(q, slot):
        return pltpu.make_async_copy(
            gu_hbm.at[pl.ds(pl.multiple_of(q * ACT_ROWS, ACT_ROWS), ACT_ROWS), :], gubuf.at[slot], gu_sem.at[slot])

    load_meta().start()
    for c in range(CHUNKS):
        load(c).start()
    gu_load(0, 0).start()

    barrier = pltpu.get_barrier_semaphore()
    for d in range(1, n_in):
        pl.semaphore_signal(barrier, inc=1, device_id={"ep": z * n_in + (p + d) % n_in}, device_id_type=MESH)

    @pl.when(z > 0)
    def _():
        pl.semaphore_signal(barrier, inc=1, device_id={"ep": e - n_in}, device_id_type=MESH)

    @pl.when(z < LINE - 1)
    def _():
        pl.semaphore_signal(barrier, inc=1, device_id={"ep": e + n_in}, device_id_type=MESH)

    pl.semaphore_wait(barrier, n_in + m)

    def zcopy(c, zd, way):
        ref = metas.at[zd] if c == CHUNKS else tok.at[c, zd]
        return pltpu.make_async_remote_copy(
            src_ref=ref, dst_ref=ref, send_sem=zsend.at[way, c, zd], recv_sem=zrecv.at[c, zd],
            device_id={"ep": e + (n_in if way else -n_in)}, device_id_type=MESH)

    def each_hop(c, zd, act):
        parts = [CHUNKS, 0] if c == 0 else [c]

        @pl.when((zd <= z) & (z < LINE - 1))
        def _():
            for part in parts:
                act(zcopy(part, zd, 1))

        @pl.when((zd >= z) & (z > 0))
        def _():
            for part in parts:
                act(zcopy(part, zd, 0))

    def own_start(c):
        if c == 0:
            load_meta().wait()
        load(c).wait()
        each_hop(c, z, lambda copy: copy.start())

    def gcopy(c, i, d):
        zd = order[i]
        src = zd * n_in + p
        return pltpu.make_async_remote_copy(
            src_ref=outb.at[c, i, d],
            dst_ref=inb.at[c, :, pl.ds(pl.multiple_of(src * per_src, 16), per_src), :],
            send_sem=gsend.at[c, i, d], recv_sem=grecv.at[c, i, d],
            device_id={"ep": z * n_in + lax.rem(p + d, n_in)}, device_id_type=MESH)

    def lcopy(c, i):
        src = order[i] * n_in + p
        return pltpu.make_async_copy(
            outb.at[c, i, 0],
            inb.at[c, :, pl.ds(pl.multiple_of(src * per_src, 16), per_src), :], lsem.at[c, i])

    def step(c, i):
        zd = order[i]
        if i == 0:
            if c == 0:
                own_start(0)
        else:
            zcopy(c, zd, 0).wait_recv()
            if c == 0:
                zcopy(CHUNKS, zd, 0).wait_recv()
            each_hop(c, zd, lambda copy: copy.start())
        if i == 2 and c + 1 < CHUNKS:
            own_start(c + 1)

        def body(d, carry):
            pp = lax.rem(p + d, n_in)
            rows = pl.ds(pl.multiple_of(pp * block, 16), block)
            if c == 0:
                first = ((z * n_in + pp) * block).astype(jnp.float32)
                ids = lax.broadcasted_iota(jnp.int32, (block, tokens), 0).astype(jnp.float32) + first
                weights = jnp.zeros((block, tokens), jnp.float32)
                for k in range(top):
                    code = metas[zd, k:k + 1, :]
                    prob = metas[zd, top + k:top + k + 1, :]
                    weights += jnp.where(ids == code, prob, 0.0)
                sel[zd, rows, :] = jnp.where(weights != 0.0, 1.0, 0.0).astype(jnp.bfloat16)
                wgt[zd, rows, :] = jnp.broadcast_to(
                    jnp.sum(weights, axis=1, keepdims=True), (block, wgt.shape[2]))
            picked = jnp.dot(sel[zd, rows, :], tok[c, zd], preferred_element_type=jnp.float32)
            scaled = (picked * wgt[zd, rows, 0:1]).astype(jnp.bfloat16)
            outb[c, i, d] = scaled.reshape(2, per_src, cols)

            @pl.when(d > 0)
            def _():
                gcopy(c, i, d).start()

            return carry

        lax.fori_loop(0, n_in, body, 0)
        lcopy(c, i).start()

    def make_act():
        def body(q, carry):
            slot = q % 2
            gu_load(q, slot).wait()

            @pl.when(q + 1 < 2 * cap // ACT_ROWS)
            def _():
                gu_load(q + 1, 1 - slot).start()

            gate = gubuf[slot, :, :hidden].astype(jnp.float32)
            up = gubuf[slot, :, hidden:].astype(jnp.float32)
            act = (gate / (1.0 + jnp.exp(-gate)) * up).astype(jnp.bfloat16)
            s = q // (cap // ACT_ROWS)
            r = q % (cap // ACT_ROWS)
            act_t[s, :, pl.ds(pl.multiple_of(r * ACT_ROWS, ACT_ROWS), ACT_ROWS)] = act.T
            return carry

        lax.fori_loop(0, 2 * cap // ACT_ROWS, body, 0)

    def finish(c):
        for i in range(LINE):
            lcopy(c, i).wait()
            for d in range(1, n_in):
                gcopy(c, i, d).wait_recv()
        piece = 256

        def body(t, carry):
            s = t // (hidden // piece)
            r = t % (hidden // piece)
            rows = pl.ds(pl.multiple_of(r * piece, piece), piece)
            tile = jnp.dot(act_t[s, rows, :], inb[c, s], preferred_element_type=jnp.float32)
            tiles_ref[s, rows, c * cols:(c + 1) * cols] = tile.astype(jnp.bfloat16)
            return carry

        lax.fori_loop(0, 2 * (hidden // piece), body, 0)

    for c in range(CHUNKS):
        for i in range(LINE):
            step(c, i)
            if c == 0 and i == 0:
                make_act()
            if c > 0 and i == 1:
                finish(c - 1)
    finish(CHUNKS - 1)

    for c in range(CHUNKS):
        for i in range(LINE):
            each_hop(c, order[i], lambda copy: copy.wait_send())
            for d in range(1, n_in):
                gcopy(c, i, d).wait_send()


def make_tiles(meta, out_grad, gate_up, n_ep, top):
    tokens, width = out_grad.shape
    cap = gate_up.shape[0] // 2
    hidden = gate_up.shape[1] // 2
    per_src = cap // n_ep
    n_in = n_ep // LINE
    cols = width // CHUNKS
    block = 2 * per_src
    return pl.pallas_call(
        functools.partial(dispatch_kernel, n_in, per_src, top),
        out_shape=jax.ShapeDtypeStruct((2, hidden, width), jnp.bfloat16),
        in_specs=[pl.BlockSpec(memory_space=pl.ANY)] * 3,
        out_specs=pl.BlockSpec(memory_space=pltpu.VMEM),
        scratch_shapes=[
            pltpu.VMEM((CHUNKS, LINE, tokens, cols), jnp.bfloat16),
            pltpu.VMEM((LINE, 2 * top, tokens), jnp.float32),
            pltpu.VMEM((LINE, n_in * block, tokens), jnp.bfloat16),
            pltpu.VMEM((LINE, n_in * block, 128), jnp.float32),
            pltpu.VMEM((CHUNKS, LINE, n_in, 2, per_src, cols), jnp.bfloat16),
            pltpu.VMEM((CHUNKS, 2, cap, cols), jnp.bfloat16),
            pltpu.VMEM((2, hidden, cap), jnp.bfloat16),
            pltpu.VMEM((2, ACT_ROWS, 2 * hidden), jnp.bfloat16),
            pltpu.SemaphoreType.DMA((CHUNKS + 1,)),
            pltpu.SemaphoreType.DMA((2,)),
            pltpu.SemaphoreType.DMA((2, CHUNKS + 1, LINE)),
            pltpu.SemaphoreType.DMA((CHUNKS + 1, LINE)),
            pltpu.SemaphoreType.DMA((CHUNKS, LINE, n_in)),
            pltpu.SemaphoreType.DMA((CHUNKS, LINE, n_in)),
            pltpu.SemaphoreType.DMA((CHUNKS, LINE)),
        ],
        compiler_params=pltpu.CompilerParams(
            collective_id=0, has_side_effects=True, vmem_limit_bytes=66 * 1000 * 1000),
    )(meta, out_grad, gate_up)


def on_device(out_grad, probs, dest, replica_owner, gate_up):
    n_ep = lax.axis_size("ep")
    n_grp = lax.axis_size("grp")
    width = out_grad.shape[1]
    top = probs.shape[1]
    cap = gate_up.shape[0] // 2
    hidden = gate_up.shape[1] // 2
    per_src = cap // n_ep
    code = (dest // cap) * per_src + dest % per_src
    code = jnp.where(dest >= 0, code, -1)
    meta = jnp.concatenate([code.T.astype(jnp.float32), probs.T], axis=0)
    tiles = make_tiles(meta, out_grad, gate_up, n_ep, top)

    owners = lax.all_gather(replica_owner[0], "grp")
    experts = jnp.arange(n_ep, dtype=jnp.int32)
    mine = lax.all_to_all(tiles.reshape(2 * hidden, width), "grp", split_axis=1, concat_axis=0, tiled=True)
    part = width // n_grp
    mine = mine.reshape(n_grp, 2, hidden, part)
    primary = jnp.sum(mine[:, 0].astype(jnp.float32), axis=0)
    pieces = lax.all_to_all(
        mine[:, 1].reshape(n_grp, n_ep, hidden // n_ep, part), "ep", split_axis=1, concat_axis=1, tiled=True)
    pieces = pieces.reshape(n_grp * n_ep, -1)
    select = (owners.reshape(-1)[None, :] == experts[:, None]).astype(jnp.bfloat16)
    sums = jnp.dot(select, pieces, preferred_element_type=jnp.float32).astype(jnp.bfloat16)
    sums = sums.reshape(-1, part)
    owned = lax.all_to_all(sums, "ep", split_axis=0, concat_axis=0, tiled=True)
    return (owned.astype(jnp.float32) + primary)[None]


def solution(mesh):
    in_specs = (
        P(("grp", "ep"), None),
        P(("grp", "ep"), None),
        P(("grp", "ep"), None),
        P("grp", None),
        P(("grp", "ep"), None),
    )
    out_specs = P("ep", None, "grp")
    return jax.shard_map(
        on_device, mesh=mesh, in_specs=in_specs, out_specs=out_specs, check_vma=False
    )
```

```python
import functools

import jax
import jax.numpy as jnp
from jax import lax
from jax.experimental import pallas as pl
from jax.experimental.pallas import tpu as pltpu
from jax.sharding import PartitionSpec as P

MESH = pl.DeviceIdType.MESH
LINE = 4
CHUNKS = 2
ACT_ROWS = 128


def dispatch_kernel(
    n_ep, n_grp, per_src, top,
    owners, meta_hbm, og_hbm, gu_hbm, out_ref,
    tok, metas, sel, wgt, outb, inb, act_t, gubuf,
    tiles, mine, pieces, sums, back,
    ld_sem, gu_sem, zsend, zrecv, gsend, grecv,
    asend, arecv, bsend, brecv, dsend, drecv,
):
    n_in = n_ep // LINE
    g = lax.axis_index("grp")
    e = lax.axis_index("ep")
    share = mine.shape[5]
    share_cols = pl.ds(pl.multiple_of(g * share, 128), share)
    z = e // n_in
    p = e % n_in
    cols = tok.shape[3]
    hidden = act_t.shape[1]
    cap = act_t.shape[2]
    block = 2 * per_src
    tokens = tok.shape[2]

    m = ((z + 1) // 2) % 2
    far, rev = (z + 2) % 4, 3 - z
    order = [z, z + 1 - 2 * (z % 2), (1 - m) * far + m * rev, (1 - m) * rev + m * far]

    def load(c, part):
        return pltpu.make_async_copy(
            og_hbm.at[:, pl.ds((part * CHUNKS + c) * share, share)],
            tok.at[c, z, :, pl.ds(part * share, share)], ld_sem.at[c, part])

    def load_meta():
        return pltpu.make_async_copy(meta_hbm, metas.at[z], ld_sem.at[CHUNKS, 0])

    def gu_load(q, slot):
        return pltpu.make_async_copy(
            gu_hbm.at[pl.ds(pl.multiple_of(q * ACT_ROWS, ACT_ROWS), ACT_ROWS), :], gubuf.at[slot], gu_sem.at[slot])

    load_meta().start()
    for c in range(CHUNKS):
        for part in range(n_grp):
            load(c, part).start()
    gu_load(0, 0).start()

    barrier = pltpu.get_barrier_semaphore()
    def greet(d, carry):
        pl.semaphore_signal(barrier, inc=1, device_id={"ep": lax.rem(e + d, n_ep)}, device_id_type=MESH)
        return carry

    lax.fori_loop(1, n_ep, greet, 0)
    for d in range(1, n_grp):
        pl.semaphore_signal(barrier, inc=1, device_id={"grp": lax.rem(g + d, n_grp)}, device_id_type=MESH)
    pl.semaphore_wait(barrier, n_ep + n_grp - 2)

    def zcopy(c, zd, way):
        ref = metas.at[zd] if c == CHUNKS else tok.at[c, zd]
        return pltpu.make_async_remote_copy(
            src_ref=ref, dst_ref=ref, send_sem=zsend.at[way, c, zd], recv_sem=zrecv.at[c, zd],
            device_id={"ep": e + (n_in if way else -n_in)}, device_id_type=MESH)

    def each_hop(c, zd, act):
        parts = [CHUNKS, 0] if c == 0 else [c]

        @pl.when((zd <= z) & (z < LINE - 1))
        def _():
            for part in parts:
                act(zcopy(part, zd, 1))

        @pl.when((zd >= z) & (z > 0))
        def _():
            for part in parts:
                act(zcopy(part, zd, 0))

    def own_start(c):
        if c == 0:
            load_meta().wait()
        for part in range(n_grp):
            load(c, part).wait()
        each_hop(c, z, lambda copy: copy.start())

    def gcopy(c, i, d):
        zd = order[i]
        src = zd * n_in + p
        return pltpu.make_async_remote_copy(
            src_ref=outb.at[c, i, d - 1],
            dst_ref=inb.at[c, :, pl.ds(pl.multiple_of(src * per_src, 16), per_src), :],
            send_sem=gsend.at[c, i, d - 1], recv_sem=grecv.at[c, i, d - 1],
            device_id={"ep": z * n_in + lax.rem(p + d, n_in)}, device_id_type=MESH)

    def step(c, i):
        zd = order[i]
        if i == 0:
            if c == 0:
                own_start(0)
        else:
            zcopy(c, zd, 0).wait_recv()
            if c == 0:
                zcopy(CHUNKS, zd, 0).wait_recv()
            each_hop(c, zd, lambda copy: copy.start())
        if i == 2 and c + 1 < CHUNKS:
            own_start(c + 1)

        def body(d, carry):
            pp = lax.rem(p + d, n_in)
            rows = pl.ds(pl.multiple_of(pp * block, 16), block)
            if c == 0:
                first = ((z * n_in + pp) * block).astype(jnp.float32)
                ids = lax.broadcasted_iota(jnp.int32, (block, tokens), 0).astype(jnp.float32) + first
                weights = jnp.zeros((block, tokens), jnp.float32)
                for k in range(top):
                    code = metas[zd, k:k + 1, :]
                    prob = metas[zd, top + k:top + k + 1, :]
                    weights += jnp.where(ids == code, prob, 0.0)
                sel[zd, rows, :] = jnp.where(weights != 0.0, 1.0, 0.0).astype(jnp.bfloat16)
                wgt[zd, rows, :] = jnp.broadcast_to(
                    jnp.sum(weights, axis=1, keepdims=True), (block, wgt.shape[2]))
            picked = jnp.dot(sel[zd, rows, :], tok[c, zd], preferred_element_type=jnp.float32)
            scaled = (picked * wgt[zd, rows, 0:1]).astype(jnp.bfloat16)
            scaled = scaled.reshape(2, per_src, cols)

            @pl.when(d == 0)
            def _():
                own = pl.ds(pl.multiple_of((zd * n_in + p) * per_src, 16), per_src)
                inb[c, :, own, :] = scaled

            @pl.when(d > 0)
            def _():
                outb[c, i, d - 1] = scaled
                gcopy(c, i, d).start()

            return carry

        lax.fori_loop(0, n_in, body, 0)

    def make_act():
        def body(q, carry):
            slot = q % 2
            gu_load(q, slot).wait()

            @pl.when(q + 1 < 2 * cap // ACT_ROWS)
            def _():
                gu_load(q + 1, 1 - slot).start()

            gate = gubuf[slot, :, :hidden].astype(jnp.float32)
            up = gubuf[slot, :, hidden:].astype(jnp.float32)
            act = (gate / (1.0 + jnp.exp(-gate)) * up).astype(jnp.bfloat16)
            s = q // (cap // ACT_ROWS)
            r = q % (cap // ACT_ROWS)
            act_t[s, :, pl.ds(pl.multiple_of(r * ACT_ROWS, ACT_ROWS), ACT_ROWS)] = act.T
            return carry

        lax.fori_loop(0, 2 * cap // ACT_ROWS, body, 0)

    def multiply(c, s):
        group = n_ep // LINE

        def body(r, carry):
            rows = pl.ds(pl.multiple_of(r * (hidden // LINE), 16), hidden // LINE)
            tile = jnp.dot(act_t[s, rows, :], inb[c, s], preferred_element_type=jnp.float32)
            tiles[c, s, pl.ds(r * group, group)] = tile.reshape(
                group, hidden // n_ep, cols).astype(jnp.bfloat16)
            return carry

        lax.fori_loop(0, LINE, body, 0)

    def swap(c, s, d):
        there = lax.rem(g + d, n_grp)
        return pltpu.make_async_remote_copy(
            src_ref=tiles.at[c, s, :, :, pl.ds(pl.multiple_of(there * share, 128), share)],
            dst_ref=mine.at[c, d - 1, s],
            send_sem=asend.at[c, s, d - 1], recv_sem=arecv.at[c, s, d - 1],
            device_id={"grp": there}, device_id_type=MESH)

    def spread(c, gd, d):
        there = lax.rem(e + d, n_ep)
        src = tiles.at[c, 1, there, :, share_cols] if gd == 0 else mine.at[c, gd - 1, 1, there]
        return pltpu.make_async_remote_copy(
            src_ref=src, dst_ref=pieces.at[c, gd, e],
            send_sem=bsend.at[c, gd, d], recv_sem=brecv.at[c, gd, d],
            device_id={"ep": there}, device_id_type=MESH)

    def spread_own(c, gd):
        src = tiles.at[c, 1, e, :, share_cols] if gd == 0 else mine.at[c, gd - 1, 1, e]
        return pltpu.make_async_copy(src, pieces.at[c, gd, e], bsend.at[c, gd, 0])

    def give(c, d):
        there = lax.rem(e + d, n_ep)
        return pltpu.make_async_remote_copy(
            src_ref=sums.at[c, there], dst_ref=back.at[c, e],
            send_sem=dsend.at[c, d], recv_sem=drecv.at[c, d],
            device_id={"ep": there}, device_id_type=MESH)

    def give_own(c):
        return pltpu.make_async_copy(sums.at[c, e], back.at[c, e], dsend.at[c, 0])

    def peers(act):
        def body(d, carry):
            act(d)
            return carry

        lax.fori_loop(1, n_ep, body, 0)

    def tail_a(c):
        for i in range(LINE):
            for d in range(1, n_in):
                gcopy(c, i, d).wait_recv()
        multiply(c, 1)
        for d in range(1, n_grp):
            swap(c, 1, d).start()
        peers(lambda d: spread(c, 0, d).start())
        spread_own(c, 0).start()
        multiply(c, 0)
        for d in range(1, n_grp):
            swap(c, 0, d).start()

    def tail_b(c):
        for gd in range(1, n_grp):
            swap(c, 1, gd).wait_recv()
            peers(lambda d: spread(c, gd, d).start())
            spread_own(c, gd).start()

    def tail_c(c):
        for gd in range(n_grp):
            spread_own(c, gd).wait()
            peers(lambda d: spread(c, gd, d).wait_recv())
        batch = 4
        height = hidden // n_ep

        def body(t, carry):
            lane = pl.ds(pl.multiple_of((t // (n_ep // batch)) * 128, 128), 128)
            first = (t % (n_ep // batch)) * batch

            def add(j, totals):
                for gd in range(n_grp):
                    owner = owners[lax.rem(g + n_grp - gd, n_grp), j]
                    piece = pieces[c, gd, j, :, lane].astype(jnp.float32)
                    totals = tuple(
                        total + piece * jnp.where(owner == first + b, 1.0, 0.0)
                        for b, total in enumerate(totals))
                return totals

            totals = lax.fori_loop(
                0, n_ep, add, tuple(jnp.zeros((height, 128), jnp.float32) for _ in range(batch)))
            for b in range(batch):
                sums[c, first + b, :, lane] = totals[b].astype(jnp.bfloat16)
            return carry

        lax.fori_loop(0, (share // 128) * (n_ep // batch), body, 0)
        peers(lambda d: give(c, d).start())
        give_own(c).start()

    def tail_d(c):
        for d in range(1, n_grp):
            swap(c, 0, d).wait_recv()
        give_own(c).wait()
        peers(lambda d: give(c, d).wait_recv())

        def body(r, carry):
            total = tiles[c, 0, r, :, share_cols].astype(jnp.float32)
            for gd in range(1, n_grp):
                total += mine[c, gd - 1, 0, r].astype(jnp.float32)
            out_ref[r, :, c * share:(c + 1) * share] = total + back[c, r].astype(jnp.float32)
            return carry

        lax.fori_loop(0, n_ep, body, 0)

    for c in range(CHUNKS):
        for i in range(LINE):
            step(c, i)
            if c == 0 and i == 0:
                make_act()
            if c > 0 and i == 0:
                tail_a(c - 1)
            if c > 0 and i == 1:
                tail_b(c - 1)
            if c > 0 and i == LINE - 1:
                tail_c(c - 1)
    tail_a(CHUNKS - 1)
    tail_b(CHUNKS - 1)
    for c in range(CHUNKS - 1):
        tail_d(c)
    tail_c(CHUNKS - 1)
    tail_d(CHUNKS - 1)

    for c in range(CHUNKS):
        for i in range(LINE):
            each_hop(c, order[i], lambda copy: copy.wait_send())
            for d in range(1, n_in):
                gcopy(c, i, d).wait_send()
        for d in range(1, n_grp):
            swap(c, 0, d).wait_send()
            swap(c, 1, d).wait_send()
        for gd in range(n_grp):
            peers(lambda d: spread(c, gd, d).wait_send())
        peers(lambda d: give(c, d).wait_send())


def run_kernel(owners, meta, out_grad, gate_up, n_ep, n_grp, top):
    tokens, width = out_grad.shape
    cap = gate_up.shape[0] // 2
    hidden = gate_up.shape[1] // 2
    per_src = cap // n_ep
    n_in = n_ep // LINE
    cols = width // CHUNKS
    share = cols // n_grp
    height = hidden // n_ep
    block = 2 * per_src
    bf16 = jnp.bfloat16
    dma = pltpu.SemaphoreType.DMA
    return pl.pallas_call(
        functools.partial(dispatch_kernel, n_ep, n_grp, per_src, top),
        out_shape=jax.ShapeDtypeStruct((n_ep, height, width // n_grp), jnp.float32),
        in_specs=[pl.BlockSpec(memory_space=pltpu.SMEM)] + [pl.BlockSpec(memory_space=pl.ANY)] * 3,
        out_specs=pl.BlockSpec(memory_space=pltpu.VMEM),
        scratch_shapes=[
            pltpu.VMEM((CHUNKS, LINE, tokens, cols), bf16),
            pltpu.VMEM((LINE, 2 * top, tokens), jnp.float32),
            pltpu.VMEM((LINE, n_in * block, tokens), bf16),
            pltpu.VMEM((LINE, n_in * block, 128), jnp.float32),
            pltpu.VMEM((CHUNKS, LINE, n_in - 1, 2, per_src, cols), bf16),
            pltpu.VMEM((CHUNKS, 2, cap, cols), bf16),
            pltpu.VMEM((2, hidden, cap), bf16),
            pltpu.VMEM((2, ACT_ROWS, 2 * hidden), bf16),
            pltpu.VMEM((CHUNKS, 2, n_ep, height, cols), bf16),
            pltpu.VMEM((CHUNKS, n_grp - 1, 2, n_ep, height, share), bf16),
            pltpu.VMEM((CHUNKS, n_grp, n_ep, height, share), bf16),
            pltpu.VMEM((CHUNKS, n_ep, height, share), bf16),
            pltpu.VMEM((CHUNKS, n_ep, height, share), bf16),
            dma((CHUNKS + 1, n_grp)),
            dma((2,)),
            dma((2, CHUNKS + 1, LINE)),
            dma((CHUNKS + 1, LINE)),
            dma((CHUNKS, LINE, n_in - 1)),
            dma((CHUNKS, LINE, n_in - 1)),
            dma((CHUNKS, 2, n_grp - 1)),
            dma((CHUNKS, 2, n_grp - 1)),
            dma((CHUNKS, n_grp, n_ep)),
            dma((CHUNKS, n_grp, n_ep)),
            dma((CHUNKS, n_ep)),
            dma((CHUNKS, n_ep)),
        ],
        compiler_params=pltpu.CompilerParams(
            collective_id=0, has_side_effects=True, vmem_limit_bytes=67043328),
    )(owners, meta, out_grad, gate_up)


def on_device(out_grad, probs, dest, replica_owner, gate_up):
    n_ep = lax.axis_size("ep")
    n_grp = lax.axis_size("grp")
    top = probs.shape[1]
    cap = gate_up.shape[0] // 2
    hidden = gate_up.shape[1] // 2
    per_src = cap // n_ep
    code = (dest // cap) * per_src + dest % per_src
    code = jnp.where(dest >= 0, code, -1)
    meta = jnp.concatenate([code.T.astype(jnp.float32), probs.T], axis=0)
    owners = lax.all_gather(replica_owner[0], "grp")
    total = run_kernel(owners, meta, out_grad, gate_up, n_ep, n_grp, top)
    return total.reshape(1, hidden, -1)


def solution(mesh):
    in_specs = (
        P(("grp", "ep"), None),
        P(("grp", "ep"), None),
        P(("grp", "ep"), None),
        P("grp", None),
        P(("grp", "ep"), None),
    )
    out_specs = P("ep", None, "grp")
    return jax.shard_map(
        on_device, mesh=mesh, in_specs=in_specs, out_specs=out_specs, check_vma=False
    )
```

```python
import functools

import jax
import jax.numpy as jnp
from jax import lax
from jax.experimental import pallas as pl
from jax.experimental.pallas import tpu as pltpu
from jax.sharding import PartitionSpec as P

MESH = pl.DeviceIdType.MESH
LINE = 4
MAX_CHUNKS = 4
NEXT_AT = 1
ACT_ROWS = 128


def dispatch_kernel(
    n_ep, n_grp, per_src, top, chunks,
    owners, meta_hbm, og_hbm, gu_hbm, out_ref,
    tok, metas, sel, wgt, outb, inb, act_t, gubuf,
    tiles, mine, pieces, sums, back,
    ld_sem, gu_sem, zsend, zrecv, gsend, grecv,
    asend, arecv, bsend, brecv, dsend, drecv,
):
    n_in = n_ep // LINE
    g = lax.axis_index("grp")
    e = lax.axis_index("ep")
    share = mine.shape[5]
    share_cols = pl.ds(pl.multiple_of(g * share, 128), share)
    z = e // n_in
    p = e % n_in
    cols = tok.shape[3]
    hidden = act_t.shape[1]
    cap = act_t.shape[2]
    block = 2 * per_src
    tokens = tok.shape[2]

    m = ((z + 1) // 2) % 2
    far, rev = (z + 2) % 4, 3 - z
    order = [z, z + 1 - 2 * (z % 2), (1 - m) * far + m * rev, (1 - m) * rev + m * far]

    def load(c, part):
        return pltpu.make_async_copy(
            og_hbm.at[:, pl.ds((part * chunks + c) * share, share)],
            tok.at[c, z, :, pl.ds(part * share, share)], ld_sem.at[c, part])

    def load_meta():
        return pltpu.make_async_copy(meta_hbm, metas.at[z], ld_sem.at[chunks, 0])

    def gu_load(q, slot):
        return pltpu.make_async_copy(
            gu_hbm.at[pl.ds(pl.multiple_of(q * ACT_ROWS, ACT_ROWS), ACT_ROWS), :], gubuf.at[slot], gu_sem.at[slot])

    load_meta().start()
    for c in range(chunks):
        for part in range(n_grp):
            load(c, part).start()
    gu_load(0, 0).start()

    barrier = pltpu.get_barrier_semaphore()
    def greet(d, carry):
        pl.semaphore_signal(barrier, inc=1, device_id={"ep": lax.rem(e + d, n_ep)}, device_id_type=MESH)
        return carry

    lax.fori_loop(1, n_ep, greet, 0)
    for d in range(1, n_grp):
        pl.semaphore_signal(barrier, inc=1, device_id={"grp": lax.rem(g + d, n_grp)}, device_id_type=MESH)
    pl.semaphore_wait(barrier, n_ep + n_grp - 2)

    def zcopy(c, zd, way):
        ref = metas.at[zd] if c == chunks else tok.at[c, zd]
        return pltpu.make_async_remote_copy(
            src_ref=ref, dst_ref=ref, send_sem=zsend.at[way, c, zd], recv_sem=zrecv.at[c, zd],
            device_id={"ep": e + (n_in if way else -n_in)}, device_id_type=MESH)

    def each_hop(c, zd, act):
        parts = [chunks, 0] if c == 0 else [c]

        @pl.when((zd <= z) & (z < LINE - 1))
        def _():
            for part in parts:
                act(zcopy(part, zd, 1))

        @pl.when((zd >= z) & (z > 0))
        def _():
            for part in parts:
                act(zcopy(part, zd, 0))

    def own_start(c):
        if c == 0:
            load_meta().wait()
        for part in range(n_grp):
            load(c, part).wait()
        each_hop(c, z, lambda copy: copy.start())

    def gcopy(c, i, d):
        zd = order[i]
        src = zd * n_in + p
        return pltpu.make_async_remote_copy(
            src_ref=outb.at[c, i, d - 1],
            dst_ref=inb.at[c, :, pl.ds(pl.multiple_of(src * per_src, 16), per_src), :],
            send_sem=gsend.at[c, i, d - 1], recv_sem=grecv.at[c, i, d - 1],
            device_id={"ep": z * n_in + lax.rem(p + d, n_in)}, device_id_type=MESH)

    def step(c, i):
        zd = order[i]
        if i == 0:
            if c == 0:
                own_start(0)
        else:
            zcopy(c, zd, 0).wait_recv()
            if c == 0:
                zcopy(chunks, zd, 0).wait_recv()
            each_hop(c, zd, lambda copy: copy.start())
        if i == NEXT_AT and c + 1 < chunks:
            own_start(c + 1)

        def body(d, carry):
            pp = lax.rem(p + d, n_in)
            rows = pl.ds(pl.multiple_of(pp * block, 16), block)
            if c == 0:
                first = ((z * n_in + pp) * block).astype(jnp.float32)
                ids = lax.broadcasted_iota(jnp.int32, (block, tokens), 0).astype(jnp.float32) + first
                weights = jnp.zeros((block, tokens), jnp.float32)
                for k in range(top):
                    code = metas[zd, k:k + 1, :]
                    prob = metas[zd, top + k:top + k + 1, :]
                    weights += jnp.where(ids == code, prob, 0.0)
                sel[zd, rows, :] = jnp.where(weights != 0.0, 1.0, 0.0).astype(jnp.bfloat16)
                wgt[zd, rows, :] = jnp.broadcast_to(
                    jnp.sum(weights, axis=1, keepdims=True), (block, wgt.shape[2]))
            picked = jnp.dot(sel[zd, rows, :], tok[c, zd], preferred_element_type=jnp.float32)
            scaled = (picked * wgt[zd, rows, 0:1]).astype(jnp.bfloat16)
            scaled = scaled.reshape(2, per_src, cols)

            @pl.when(d == 0)
            def _():
                own = pl.ds(pl.multiple_of((zd * n_in + p) * per_src, 16), per_src)
                inb[c, :, own, :] = scaled

            @pl.when(d > 0)
            def _():
                outb[c, i, d - 1] = scaled
                gcopy(c, i, d).start()

            return carry

        lax.fori_loop(0, n_in, body, 0)

    def make_act():
        def body(q, carry):
            slot = q % 2
            gu_load(q, slot).wait()

            @pl.when(q + 1 < 2 * cap // ACT_ROWS)
            def _():
                gu_load(q + 1, 1 - slot).start()

            gate = gubuf[slot, :, :hidden].astype(jnp.float32)
            up = gubuf[slot, :, hidden:].astype(jnp.float32)
            act = (gate / (1.0 + jnp.exp(-gate)) * up).astype(jnp.bfloat16)
            s = q // (cap // ACT_ROWS)
            r = q % (cap // ACT_ROWS)
            act_t[s, :, pl.ds(pl.multiple_of(r * ACT_ROWS, ACT_ROWS), ACT_ROWS)] = act.T
            return carry

        lax.fori_loop(0, 2 * cap // ACT_ROWS, body, 0)

    def multiply(c, s):
        group = n_ep // LINE

        def body(r, carry):
            rows = pl.ds(pl.multiple_of(r * (hidden // LINE), 16), hidden // LINE)
            tile = jnp.dot(act_t[s, rows, :], inb[c, s], preferred_element_type=jnp.float32)
            tiles[c, s, pl.ds(r * group, group)] = tile.reshape(
                group, hidden // n_ep, cols).astype(jnp.bfloat16)
            return carry

        lax.fori_loop(0, LINE, body, 0)

    def swap(c, s, d):
        there = lax.rem(g + d, n_grp)
        return pltpu.make_async_remote_copy(
            src_ref=tiles.at[c, s, :, :, pl.ds(pl.multiple_of(there * share, 128), share)],
            dst_ref=mine.at[c, d - 1, s],
            send_sem=asend.at[c, s, d - 1], recv_sem=arecv.at[c, s, d - 1],
            device_id={"grp": there}, device_id_type=MESH)

    def spread(c, gd, d):
        there = lax.rem(e + d, n_ep)
        src = tiles.at[c, 1, there, :, share_cols] if gd == 0 else mine.at[c, gd - 1, 1, there]
        return pltpu.make_async_remote_copy(
            src_ref=src, dst_ref=pieces.at[c, gd, e],
            send_sem=bsend.at[c, gd, d], recv_sem=brecv.at[c, gd, d],
            device_id={"ep": there}, device_id_type=MESH)

    def spread_own(c, gd):
        src = tiles.at[c, 1, e, :, share_cols] if gd == 0 else mine.at[c, gd - 1, 1, e]
        return pltpu.make_async_copy(src, pieces.at[c, gd, e], bsend.at[c, gd, 0])

    def give(c, d):
        there = lax.rem(e + d, n_ep)
        return pltpu.make_async_remote_copy(
            src_ref=sums.at[c, there], dst_ref=back.at[c, e],
            send_sem=dsend.at[c, d], recv_sem=drecv.at[c, d],
            device_id={"ep": there}, device_id_type=MESH)

    def give_own(c):
        return pltpu.make_async_copy(sums.at[c, e], back.at[c, e], dsend.at[c, 0])

    def peers(act):
        def body(d, carry):
            act(d)
            return carry

        lax.fori_loop(1, n_ep, body, 0)

    def tail_a(c):
        for i in range(LINE):
            for d in range(1, n_in):
                gcopy(c, i, d).wait_recv()
        multiply(c, 1)
        for d in range(1, n_grp):
            swap(c, 1, d).start()
        peers(lambda d: spread(c, 0, d).start())
        spread_own(c, 0).start()
        multiply(c, 0)
        for d in range(1, n_grp):
            swap(c, 0, d).start()

    def tail_b(c):
        for gd in range(1, n_grp):
            swap(c, 1, gd).wait_recv()
            peers(lambda d: spread(c, gd, d).start())
            spread_own(c, gd).start()

    def tail_c(c):
        for gd in range(n_grp):
            spread_own(c, gd).wait()
            peers(lambda d: spread(c, gd, d).wait_recv())
        batch = 4
        height = hidden // n_ep

        def body(t, carry):
            lane = pl.ds(pl.multiple_of((t // (n_ep // batch)) * 128, 128), 128)
            first = (t % (n_ep // batch)) * batch

            def add(j, totals):
                for gd in range(n_grp):
                    owner = owners[lax.rem(g + n_grp - gd, n_grp), j]
                    piece = pieces[c, gd, j, :, lane].astype(jnp.float32)
                    totals = tuple(
                        total + piece * jnp.where(owner == first + b, 1.0, 0.0)
                        for b, total in enumerate(totals))
                return totals

            totals = lax.fori_loop(
                0, n_ep, add, tuple(jnp.zeros((height, 128), jnp.float32) for _ in range(batch)))
            for b in range(batch):
                sums[c, first + b, :, lane] = totals[b].astype(jnp.bfloat16)
            return carry

        lax.fori_loop(0, (share // 128) * (n_ep // batch), body, 0)
        peers(lambda d: give(c, d).start())
        give_own(c).start()

    def tail_d(c):
        for d in range(1, n_grp):
            swap(c, 0, d).wait_recv()
        give_own(c).wait()
        peers(lambda d: give(c, d).wait_recv())

        def body(r, carry):
            total = tiles[c, 0, r, :, share_cols].astype(jnp.float32)
            for gd in range(1, n_grp):
                total += mine[c, gd - 1, 0, r].astype(jnp.float32)
            out_ref[r, :, c * share:(c + 1) * share] = total + back[c, r].astype(jnp.float32)
            return carry

        lax.fori_loop(0, n_ep, body, 0)

    for c in range(chunks):
        for i in range(LINE):
            step(c, i)
            if c == 0 and i == 0:
                make_act()
            if c > 0 and i == 0:
                tail_a(c - 1)
            if c > 0 and i == 1:
                tail_b(c - 1)
            if c > 1 and i == 1:
                tail_c(c - 2)
    tail_a(chunks - 1)
    tail_b(chunks - 1)
    if chunks > 1:
        tail_c(chunks - 2)
    for c in range(chunks - 1):
        tail_d(c)
    tail_c(chunks - 1)
    tail_d(chunks - 1)

    for c in range(chunks):
        for i in range(LINE):
            each_hop(c, order[i], lambda copy: copy.wait_send())
            for d in range(1, n_in):
                gcopy(c, i, d).wait_send()
        for d in range(1, n_grp):
            swap(c, 0, d).wait_send()
            swap(c, 1, d).wait_send()
        for gd in range(n_grp):
            peers(lambda d: spread(c, gd, d).wait_send())
        peers(lambda d: give(c, d).wait_send())


def run_kernel(owners, meta, out_grad, gate_up, n_ep, n_grp, top):
    tokens, width = out_grad.shape
    cap = gate_up.shape[0] // 2
    hidden = gate_up.shape[1] // 2
    per_src = cap // n_ep
    n_in = n_ep // LINE
    chunks = max(1, min(MAX_CHUNKS, width // n_grp // 128))
    cols = width // chunks
    share = cols // n_grp
    height = hidden // n_ep
    block = 2 * per_src
    bf16 = jnp.bfloat16
    dma = pltpu.SemaphoreType.DMA
    return pl.pallas_call(
        functools.partial(dispatch_kernel, n_ep, n_grp, per_src, top, chunks),
        out_shape=jax.ShapeDtypeStruct((n_ep, height, width // n_grp), jnp.float32),
        in_specs=[pl.BlockSpec(memory_space=pltpu.SMEM)] + [pl.BlockSpec(memory_space=pl.ANY)] * 3,
        out_specs=pl.BlockSpec(memory_space=pltpu.VMEM),
        scratch_shapes=[
            pltpu.VMEM((chunks, LINE, tokens, cols), bf16),
            pltpu.VMEM((LINE, 2 * top, tokens), jnp.float32),
            pltpu.VMEM((LINE, n_in * block, tokens), bf16),
            pltpu.VMEM((LINE, n_in * block, 128), jnp.float32),
            pltpu.VMEM((chunks, LINE, n_in - 1, 2, per_src, cols), bf16),
            pltpu.VMEM((chunks, 2, cap, cols), bf16),
            pltpu.VMEM((2, hidden, cap), bf16),
            pltpu.VMEM((2, ACT_ROWS, 2 * hidden), bf16),
            pltpu.VMEM((chunks, 2, n_ep, height, cols), bf16),
            pltpu.VMEM((chunks, n_grp - 1, 2, n_ep, height, share), bf16),
            pltpu.VMEM((chunks, n_grp, n_ep, height, share), bf16),
            pltpu.VMEM((chunks, n_ep, height, share), bf16),
            pltpu.VMEM((chunks, n_ep, height, share), bf16),
            dma((chunks + 1, n_grp)),
            dma((2,)),
            dma((2, chunks + 1, LINE)),
            dma((chunks + 1, LINE)),
            dma((chunks, LINE, n_in - 1)),
            dma((chunks, LINE, n_in - 1)),
            dma((chunks, 2, n_grp - 1)),
            dma((chunks, 2, n_grp - 1)),
            dma((chunks, n_grp, n_ep)),
            dma((chunks, n_grp, n_ep)),
            dma((chunks, n_ep)),
            dma((chunks, n_ep)),
        ],
        compiler_params=pltpu.CompilerParams(
            collective_id=0, has_side_effects=True, vmem_limit_bytes=67043328),
    )(owners, meta, out_grad, gate_up)


def on_device(out_grad, probs, dest, replica_owner, gate_up):
    n_ep = lax.axis_size("ep")
    n_grp = lax.axis_size("grp")
    top = probs.shape[1]
    cap = gate_up.shape[0] // 2
    hidden = gate_up.shape[1] // 2
    per_src = cap // n_ep
    code = (dest // cap) * per_src + dest % per_src
    code = jnp.where(dest >= 0, code, -1)
    meta = jnp.concatenate([code.T.astype(jnp.float32), probs.T], axis=0)
    owners = lax.all_gather(replica_owner[0], "grp")
    total = run_kernel(owners, meta, out_grad, gate_up, n_ep, n_grp, top)
    return total.reshape(1, hidden, -1)


def solution(mesh):
    in_specs = (
        P(("grp", "ep"), None),
        P(("grp", "ep"), None),
        P(("grp", "ep"), None),
        P("grp", None),
        P(("grp", "ep"), None),
    )
    out_specs = P("ep", None, "grp")
    return jax.shard_map(
        on_device, mesh=mesh, in_specs=in_specs, out_specs=out_specs, check_vma=False
    )
```
